32 devices in a mesh: groups: 2 (over x), wide: 16 (over z, y, core).
Axes of the slice: x: 2, y: 2, z: 4, core: 2. Of those that a mesh axis runs over, the one named last changes fastest.
Arguments:
- iterate: float32 [8192, 128], P(('groups', 'wide')), parts along dimension 0, may hold values from -6 to 6
- rhs: float32 [8192, 128], P(('groups', 'wide')), parts along dimension 0, may hold values from -6 to 6
- schur: float32 [32, 384, 384], P(('groups', 'wide')), parts along dimension 0
- near_block: float32 [8192, 256], P(('groups', 'wide')), parts along dimension 0
- u_basis: float32 [32, 32, 4096], P('groups', None, 'wide'), parts along dimension 0, may hold values from -0.375 to 0.375
- v_basis: float32 [32, 32, 4096], P('groups', None, 'wide'), parts along dimension 0, may hold values from -0.375 to 0.375
- tile_rank: int32 [32, 16], P('groups', 'wide'), parts along dimension 0, may hold values from 1 to 32
- send_rows: int32 [32, 3, 128], P(('groups', 'wide')), parts along dimension 0, may hold values from 0 to 255
- send_count: int32 [32, 3], P(('groups', 'wide')), parts along dimension 0, may hold values from 0 to 128, as said below
- precond: float32 [8192], P(('groups', 'wide')), parts along dimension 0, may hold values from 0.1 to 1
Outputs:
- updated: float32 [8192, 128], P(('groups', 'wide')), parts along dimension 0
- residual: float32 [8192, 128], P(('groups', 'wide')), parts along dimension 0
The draws below stay inside these ranges and needn't reach their ends.
There are 2 independent parts, one for each index of `groups`. The reference program is written for one: setup_inputs(seed, part) draws one part's arguments, and reference() takes and returns one part's arrays. A program takes and returns all parts, laid end to end along the dimension named above; each array names one. Nothing has to cross between parts.
Inputs may be any that keep to these rules, and one draw needn't show every extreme that they name: send_count[p, 0] is 0 for p = 0 and send_count[p, 2] is 0 for p = 15; a block is full in every draw.
All inputs are finite; a program needn't handle non-finite values.
Results may differ from the reference program's by a relative error of at most 0.0003.
Values sent between devices are 32-bit elements; how exact they have to be, the bound alone decides.
A program may use at most 64 MiB of HBM per device.

```python
import math
import jax
import jax.numpy as jnp
from jax import lax

R_DEV = 256
LOADS = 128
K = 32
FB = 128
NS = 384
TILES = 16
N = 4096


def draw_schur(key, part):
    key_off = jax.random.fold_in(key, 11)
    key_diag = jax.random.fold_in(key, 12)
    off_diag = jax.random.normal(key_off, (TILES, NS, NS), jnp.float32)
    off_diag = off_diag * (0.5 / jnp.sqrt(jnp.float32(NS)))
    diag = jax.random.uniform(key_diag, (TILES, NS), jnp.float32, 1.5, 3.0)
    return off_diag + diag[:, :, None] * jnp.eye(NS, dtype=jnp.float32)[None]


def draw_near_block(key, part):
    key_off = jax.random.fold_in(key, 21)
    key_diag = jax.random.fold_in(key, 22)
    off_diag = jax.random.normal(key_off, (N, R_DEV), jnp.float32)
    off_diag = off_diag * (0.5 / jnp.sqrt(jnp.float32(R_DEV)))
    diag = jax.random.uniform(key_diag, (N, 1), jnp.float32, 0.5, 1.5)
    eye_rows = jnp.tile(jnp.eye(R_DEV, dtype=jnp.float32), (TILES, 1))
    return off_diag + diag * eye_rows


def draw_tile_rank(key, part):
    ranks = jax.random.randint(jax.random.fold_in(key, 31), (TILES, TILES), 1, K + 1, dtype=jnp.int32)
    return ranks.at[0, 1].set(1).at[1, 0].set(K)


def draw_send_count(key, part):
    counts = jax.random.randint(jax.random.fold_in(key, 41), (TILES, 3), 0, FB + 1, dtype=jnp.int32)
    owner = jnp.arange(TILES, dtype=jnp.int32)[:, None]
    offset = jnp.arange(3, dtype=jnp.int32)[None, :] - 1
    target = owner + offset
    inside = (target >= 0) & (target < TILES)
    counts = jnp.where(inside, counts, 0)
    return counts.at[1, 1].set(FB)


def touch_ends(drawn, stream_key, low, high):
    longest = drawn.shape.index(max(drawn.shape))
    spots = []
    for shift in (0, 1):
        where = [jax.random.randint(jax.random.fold_in(stream_key, axis), (), 0, length) for axis, length in enumerate(drawn.shape)]
        where[longest] = (where[longest] + shift) % drawn.shape[longest]
        spots.append(tuple(where))
    return drawn.at[spots[0]].set(low).at[spots[1]].set(high)


def raised(drawn, key, source, target, parts, factor):
    def block_of(axis_at):
        return (jnp.arange(drawn.shape[axis_at]) // (drawn.shape[axis_at] // parts)).reshape((-1,) + (1,) * (drawn.ndim - 1 - axis_at))

    one_side = jax.random.permutation(key, parts)[block_of(target)]
    second = (block_of(target) + parts // 2) % parts
    return jnp.where((block_of(source) == one_side) | (block_of(source) == second), factor * drawn, drawn)


def block_scale(rng, shape, shards, smallest, high):
    factor_of = 1.0
    for dim, blocks in shards:
        heights = jax.random.uniform(jax.random.fold_in(jax.random.fold_in(rng, 6), dim), (blocks,), jnp.float32, smallest / len(shards), high / len(shards))
        factor_of = factor_of * jnp.repeat(jnp.exp(heights), shape[dim] // blocks).reshape((-1,) + (1,) * (len(shape) - 1 - dim))
    return factor_of


def scatter_about(rng, shape, width, limit, split=(), kind=jnp.bfloat16):
    result = jax.random.normal(rng, shape, jnp.float32) * width
    if len(split) > 0:
        result = block_scale(rng, shape, split, -0.22, 0.18) * result
    return jnp.clip(result, min=-limit, max=limit).astype(kind)


def noise_with(stream_key, extent, spread, bound, split, heavy, held_as=jnp.bfloat16):
    entries = spread * jax.random.normal(stream_key, extent, jnp.float32)
    if split:
        entries = entries * block_scale(stream_key, extent, split, -0.22, 0.18)
    return jnp.clip(raised(entries, jax.random.fold_in(stream_key, 3), *heavy), -bound, bound).astype(held_as)


def setup_inputs(seed: int = 0, part: int = 0) -> dict:
    splits = jax.random.split(jax.random.key(seed), 11)
    part_splits = jax.random.split(jax.random.fold_in(splits[10], part), 11)
    iterate = scatter_about(part_splits[0], (N, LOADS), 1.0, 6.0, ((0, 16),), jnp.float32)
    rhs = scatter_about(part_splits[1], (N, LOADS), 1.0, 6.0, ((0, 16),), jnp.float32)
    schur = draw_schur(jax.random.fold_in(jax.random.fold_in(splits[10], part), 71), part)
    near_block = draw_near_block(jax.random.fold_in(jax.random.fold_in(splits[10], part), 71), part)
    u_basis = noise_with(part_splits[4], (TILES, K, N), (TILES * K) ** -0.5, 0.375, ((2, 16),), (0, 2, 16, 2.0), jnp.float32)
    v_basis = scatter_about(part_splits[5], (TILES, K, N), R_DEV ** -0.5, 0.375, ((2, 16),), jnp.float32)
    tile_rank = draw_tile_rank(jax.random.fold_in(jax.random.fold_in(splits[10], part), 71), part)
    send_rows = touch_ends(jax.random.randint(part_splits[7], (TILES, 3, FB), 0, R_DEV), jax.random.fold_in(part_splits[7], 1), 0, R_DEV - 1).astype(jnp.int32)
    send_count = draw_send_count(jax.random.fold_in(jax.random.fold_in(splits[10], part), 71), part)
    precond = jnp.clip(jnp.exp(math.log(1.0) - 2.3025851 * jax.random.uniform(part_splits[9], (N,), jnp.float32) ** block_scale(part_splits[9], (N,), ((0, 16),), -0.2, 0.2)), 0.1, 1.0)
    return {"iterate": iterate, "rhs": rhs, "schur": schur, "near_block": near_block, "u_basis": u_basis, "v_basis": v_basis, "tile_rank": tile_rank, "send_rows": send_rows, "send_count": send_count, "precond": precond}


def reference(iterate, rhs, schur, near_block, u_basis, v_basis, tile_rank, send_rows, send_count, precond):
    highest = lax.Precision.HIGHEST
    rows_local = jnp.arange(R_DEV, dtype=jnp.int32)
    slot_ids = jnp.arange(FB, dtype=jnp.int32)
    blocks = iterate.reshape(TILES, R_DEV, LOADS)
    valid = slot_ids[None, None, :] < send_count[:, :, None]
    select = ((send_rows[..., None] == rows_local) & valid[..., None]).astype(iterate.dtype)
    outgoing = jnp.einsum('posr,prl->posl', select, blocks, precision=highest)
    zero_block = jnp.zeros((1, 3, FB, LOADS), iterate.dtype)
    out_pad = jnp.concatenate([zero_block, outgoing, zero_block], axis=0)
    incoming = jnp.stack([out_pad[2:, 0], out_pad[1:-1, 1], out_pad[:-2, 2]], axis=1)
    forces = jnp.einsum('dab,dbl->dal', schur, incoming.reshape(TILES, NS, LOADS), precision=highest)
    forces = forces.reshape(TILES, 3, FB, LOADS)
    force_pad = jnp.concatenate([zero_block, forces, zero_block], axis=0)
    returned = jnp.stack([force_pad[:-2, 0], force_pad[1:-1, 1], force_pad[2:, 2]], axis=1)
    fem = jnp.einsum('posr,posl->prl', select, returned, precision=highest).reshape(N, LOADS)
    rank_ids = jnp.arange(K, dtype=jnp.int32)

    def tile_row(index):
        v_row = v_basis[index].reshape(K, TILES, R_DEV)
        coeff = jnp.einsum('kjr,jrl->jkl', v_row, blocks, precision=highest)
        keep = (rank_ids[None, :] < tile_rank[index][:, None]).astype(iterate.dtype)
        coeff = coeff * keep[:, :, None]
        u_row = lax.dynamic_slice_in_dim(u_basis, index * R_DEV, R_DEV, 2)
        return jnp.einsum('jkr,jkl->rl', u_row, coeff, precision=highest)

    far = lax.map(tile_row, jnp.arange(TILES, dtype=jnp.int32)).reshape(N, LOADS)
    near = jnp.einsum('prs,psl->prl', near_block.reshape(TILES, R_DEV, R_DEV), blocks, precision=highest).reshape(N, LOADS)
    residual = rhs - (fem + (far + near))
    updated = iterate + precond[:, None] * residual
    return updated, residual
```

```python
import functools
import math

import jax
import jax.numpy as jnp
from jax import lax
from jax.experimental import pallas as pl
from jax.experimental.pallas import tpu as pltpu
from jax.sharding import PartitionSpec as P

MESH = pl.DeviceIdType.MESH
F32 = jnp.float32
BF16 = jnp.bfloat16


def halves(x):
    high = x.astype(BF16)
    low = (x - high.astype(F32)).astype(BF16)
    return high, low


def mm(a, b):
    return jnp.dot(a, b, preferred_element_type=F32)


def pair(x):
    high, low = halves(x)
    return jnp.concatenate([high, low], axis=1), high


def fold(p):
    width = p.shape[1] // 2
    return p[:, :width] + p[:, width:]


def product(a_high, a_low, b_both, b_high):
    return fold(mm(a_high, b_both)) + mm(a_low, b_high)


def kernel(
    n,
    iterate_hbm, schur_hbm, near_hbm, u_hbm, v_hbm, rank_hbm, rows_hbm, count_hbm,
    out_ref,
    iterate, schur, near, u, v, rank, rows, count,
    edge_out, in_face, in_force, sent, gathered, u_high, u_low,
    load_sem, edge_send, face_recv, force_recv, send_sem, recv_sem, late_sem,
):
    me = lax.axis_index("wide")
    loads = iterate.shape[1]
    face = rows.shape[2]
    rank_top = v.shape[1]
    rows_here = iterate.shape[0]

    blocks = 4 if n % 4 == 0 else 1
    per_block = n // blocks
    group = math.gcd(per_block, max(1, 128 // rank_top))
    chunks = per_block // group
    block = lax.div(me, per_block)
    mine = lax.div(me, group)
    place_in_block = lax.rem(me, per_block)
    place_in_group = lax.rem(me, group)

    def by_block(first, second, third, fourth):
        at_least = [lax.div(block + 2, 3), lax.div(block, 2), lax.div(block, 3)]
        return first + (second - first) * at_least[0] + (third - second) * at_least[1] + (fourth - third) * at_least[2]

    if blocks == 4:
        send_order = [by_block(1, 2, 0, 0), by_block(0, 0, 1, 1), by_block(2, 1, 2, 2), 3]
        own_slot = by_block(1, 2, 2, 3)
        recv_order = [block, by_block(1, 0, 1, 2), by_block(2, 2, 0, 1), by_block(3, 3, 3, 0)]
    else:
        send_order, own_slot, recv_order = [0], 0, [0]

    def load(at, source, target):
        copy = pltpu.make_async_copy(source, target, load_sem.at[at])
        copy.start()
        return copy

    def load_v(slot, c):
        first = send_order[slot] * per_block + c * group
        at = slot * chunks + c
        return load(7 + at, v_hbm.at[pl.ds(first, group)], v.at[pl.ds(at * group, group)])

    iterate_load = load(0, iterate_hbm, iterate)
    barrier = pltpu.get_barrier_semaphore()

    def tell(semaphore, target):
        pl.semaphore_signal(semaphore, inc=1, device_id={"wide": target}, device_id_type=MESH)

    def tell_block(semaphore, target_block):
        for k in range(per_block):
            tell(semaphore, target_block * per_block + lax.rem(place_in_block + k, per_block))

    for k in range(1, per_block):
        tell(barrier, block * per_block + lax.rem(place_in_block + k, per_block))
    if blocks == 4:
        for target in range(blocks):
            last = [1, 2, 2, 3][target]

            @pl.when(jnp.logical_and(block != target, block <= last))
            def _():
                tell_block(barrier, target)

    def enter():
        pl.semaphore_wait(barrier, (per_block * by_block(2, 3, 3, 4) if blocks == 4 else n) - 1)

    def announce():
        if blocks == 4:
            @pl.when(block == 2)
            def _():
                tell_block(late_sem.at[0], 0)

            @pl.when(block == 3)
            def _():
                for target in range(3):
                    tell_block(late_sem.at[1], target)

    def late(which):
        if blocks == 4:
            @pl.when(block == 0 if which == 0 else block < 3)
            def _():
                pl.semaphore_wait(late_sem.at[which], per_block)

    rows_load = load(2, rows_hbm, rows)
    count_load = load(3, count_hbm, count)
    rank_load = load(1, rank_hbm, rank)
    v_loads = {(slot, c): load_v(slot, c) for slot in range(blocks) for c in range(chunks)}
    near_load = load(6, near_hbm, near)
    u_load = load(5, u_hbm, u)
    schur_load = load(4, schur_hbm, schur)

    @pl.when(me == 0)
    def _():
        in_face[2] = jnp.zeros_like(in_face[2])
        in_force[0] = jnp.zeros_like(in_force[0])

    @pl.when(me == n - 1)
    def _():
        in_face[0] = jnp.zeros_like(in_face[0])
        in_force[2] = jnp.zeros_like(in_force[2])

    below, above = lax.rem(me + n - 1, n), lax.rem(me + 1, n)
    has_below, has_above = me > 0, me < n - 1

    def edge_copy(side, kind, target, recv):
        return pltpu.make_async_remote_copy(
            src_ref=edge_out.at[side, kind], dst_ref=target, send_sem=edge_send.at[side], recv_sem=recv,
            device_id={"wide": above if side else below}, device_id_type=MESH,
        )

    face_down = edge_copy(0, 0, in_face.at[0], face_recv.at[0])
    face_up = edge_copy(1, 0, in_face.at[2], face_recv.at[1])
    force_up = edge_copy(1, 1, in_force.at[0], force_recv.at[0])
    force_down = edge_copy(0, 1, in_force.at[2], force_recv.at[1])

    iterate_load.wait()
    it_both, it_high = pair(iterate[...])
    rows_load.wait()
    count_load.wait()
    slot_ids = lax.broadcasted_iota(jnp.int32, (1, face), 1)
    row_of = [jnp.where(slot_ids < count[0, o], rows[o], -1) for o in range(3)]
    lanes = lax.broadcasted_iota(jnp.int32, (face, rows_here), 1)

    def picked(o):
        column = jnp.broadcast_to(row_of[o].astype(F32), (face, face)).T[:, :1].astype(jnp.int32)
        select = (column == lanes).astype(F32).astype(BF16)
        return fold(mm(select, it_both))

    edge_out[0, 0] = picked(0)
    edge_out[1, 0] = picked(2)

    rank_ids = lax.broadcasted_iota(jnp.int32, (rank_top, loads), 0)

    def compress(slot, c):
        v_loads[slot, c].wait()
        at = (slot * chunks + c) * group
        first = send_order[slot] * per_block + c * group
        v_high, v_low = halves(v[at : at + group].reshape(group * rank_top, rows_here))
        coeff = product(v_high, v_low, it_both, it_high)
        for g in range(group):
            part = coeff[g * rank_top : (g + 1) * rank_top]
            sent[at + g] = jnp.where(rank_ids < rank[0, first + g], part, 0.0)

    paired = group & (group - 1) == 0 and group > 1
    if paired:
        offsets = [int(bin(group + k)[:2:-1], 2) for k in range(group)]
        flip = lax.rem(me, 2) * (group // 2)

    def member(k):
        if not paired:
            return lax.rem(place_in_group + k, group)
        moved = place_in_group
        for bit in [1 << b for b in range(group.bit_length() - 1)]:
            on = 1 if offsets[k] & bit else 0
            change = on + lax.rem(me, 2) - 2 * on * lax.rem(me, 2) if bit == group // 2 else on
            moved = moved + change * bit * (1 - 2 * lax.rem(lax.div(place_in_group, bit), 2))
        return moved

    def send(slot, c):
        first = send_order[slot] * per_block + c * group
        for k in range(group):
            in_group = member(k)

            def start():
                pltpu.make_async_remote_copy(
                    src_ref=sent.at[(slot * chunks + c) * group + in_group], dst_ref=gathered.at[me],
                    send_sem=send_sem.at[0], recv_sem=recv_sem.at[mine],
                    device_id={"wide": first + in_group}, device_id_type=MESH,
                ).start()

            if blocks == 4 and (slot == 0 or paired and offsets[k] not in (0, group // 2)):
                start()
            else:
                pl.when(first + in_group != me)(start)

    rank_load.wait()
    steps = [(slot, c) for slot in range(blocks) for c in range(chunks)]

    def of_slot(slot):
        return [(slot, c) for c in range(chunks)]

    compress(*steps[0])
    enter()
    announce()
    waits_above = me == 3 * per_block - 1 if blocks == 4 else me < 0

    @pl.when(has_below)
    def _():
        face_down.start()

    @pl.when(jnp.logical_and(has_above, jnp.logical_not(waits_above)))
    def _():
        face_up.start()

    send(*steps[0])
    for step in steps[1 : 2 * chunks]:
        compress(*step)
        send(*step)
    for step in steps[2 * chunks :]:
        compress(*step)
    gathered[me] = sent[own_slot * per_block + place_in_block]
    if blocks == 4:
        late(0)
        for step in of_slot(2):
            send(*step)

    in_face[1] = picked(1)
    near_load.wait()
    near_high, near_low = halves(near[...])
    out_ref[...] = product(near_high, near_low, it_both, it_high)
    u_load.wait()
    for at in range(n // group):
        high, low = halves(u[at * group : (at + 1) * group].reshape(group * rank_top, rows_here).T)
        u_high[at] = high
        u_low[at] = low

    schur_load.wait()
    s_high, s_low = halves(schur[0])

    def force_part(o):
        span = slice(o * face, (o + 1) * face)
        b_both, b_high = pair(in_face[o])
        return product(s_high[:, span], s_low[:, span], b_both, b_high)

    force = force_part(1)
    if blocks == 4:
        late(1)

        @pl.when(waits_above)
        def _():
            face_up.start()

        for step in of_slot(3):
            send(*step)

    def face_wait():
        @pl.when(has_above)
        def _():
            face_down.wait_recv()

        @pl.when(has_below)
        def _():
            face_up.wait_recv()

    face_wait()
    force = force + force_part(0) + force_part(2)
    edge_out[0, 1] = force[2 * face :]
    edge_out[1, 1] = force[:face]
    in_force[1] = force[face : 2 * face]

    @pl.when(has_above)
    def _():
        force_up.start()

    @pl.when(has_below)
    def _():
        force_down.start()

    place = lax.broadcasted_iota(jnp.int32, (rows_here, face), 0)

    def scattered(o):
        scatter = (place == row_of[o]).astype(F32).astype(BF16)
        b_both, _ = pair(in_force[o])
        return fold(mm(scatter, b_both))

    def far(slot, c):
        at = recv_order[slot] * chunks + c

        def arrived(tiles):
            span = gathered.at[pl.ds(0, tiles)]
            pltpu.make_async_remote_copy(
                src_ref=span, dst_ref=span, send_sem=send_sem.at[0], recv_sem=recv_sem.at[at],
                device_id={"wide": above}, device_id_type=MESH,
            ).wait_recv()

        def wait():
            if slot > 0:
                arrived(group)
                return
            if group > 1:
                @pl.when(at == mine)
                def _():
                    arrived(group - 1)

            if chunks > 1:
                @pl.when(at != mine)
                def _():
                    arrived(group)

        wait()
        got = gathered[pl.ds(at * group, group)].reshape(group * rank_top, loads)
        b_both, b_high = pair(got)
        return product(u_high[at], u_low[at], b_both, b_high)

    out_ref[...] += scattered(1)
    order = [(slot, c) for slot in range(blocks) for c in range(chunks)]
    for slot, c in order[:-1]:
        out_ref[...] += far(slot, c)

    def force_wait():
        @pl.when(has_below)
        def _():
            force_up.wait_recv()

        @pl.when(has_above)
        def _():
            force_down.wait_recv()

    force_wait()
    out_ref[...] += scattered(0) + scattered(2)
    out_ref[...] += far(*order[-1])

    def sent_wait():
        @pl.when(has_below)
        def _():
            pltpu.make_async_remote_copy(
                src_ref=edge_out.at[0], dst_ref=edge_out.at[0], send_sem=edge_send.at[0],
                recv_sem=face_recv.at[0], device_id={"wide": below}, device_id_type=MESH,
            ).wait_send()

        @pl.when(has_above)
        def _():
            pltpu.make_async_remote_copy(
                src_ref=edge_out.at[1], dst_ref=edge_out.at[1], send_sem=edge_send.at[1],
                recv_sem=face_recv.at[1], device_id={"wide": above}, device_id_type=MESH,
            ).wait_send()

        all_sent = sent.at[pl.ds(0, n - 1)]
        pltpu.make_async_remote_copy(
            src_ref=all_sent, dst_ref=all_sent, send_sem=send_sem.at[0], recv_sem=recv_sem.at[0],
            device_id={"wide": above}, device_id_type=MESH,
        ).wait_send()

    sent_wait()


def body(
    iterate, rhs, schur, near_block, u_basis, v_basis, tile_rank, send_rows, send_count, precond
):
    n = lax.axis_size("wide")
    rows_here, loads = iterate.shape
    face = send_rows.shape[2]
    tiles, rank_top, _ = u_basis.shape
    group = math.gcd(n // 4 if n % 4 == 0 else n, max(1, 128 // rank_top))
    tile_rank = tile_rank.reshape(1, tiles)
    send_rows = send_rows.reshape(3, 1, face)
    dma = pltpu.SemaphoreType.DMA
    applied = pl.pallas_call(
        functools.partial(kernel, n),
        out_shape=pltpu.VMEM((rows_here, loads), F32),
        in_specs=[pl.BlockSpec(memory_space=pl.ANY)] * 8,
        out_specs=pl.BlockSpec(memory_space=pltpu.VMEM),
        scratch_shapes=[
            pltpu.VMEM(iterate.shape, F32),
            pltpu.VMEM(schur.shape, F32),
            pltpu.VMEM(near_block.shape, F32),
            pltpu.VMEM(u_basis.shape, F32),
            pltpu.VMEM(v_basis.shape, F32),
            pltpu.SMEM(tile_rank.shape, jnp.int32),
            pltpu.VMEM(send_rows.shape, jnp.int32),
            pltpu.SMEM(send_count.shape, jnp.int32),
            pltpu.VMEM((2, 2, face, loads), F32),
            pltpu.VMEM((3, face, loads), F32),
            pltpu.VMEM((3, face, loads), F32),
            pltpu.VMEM((n, rank_top, loads), F32),
            pltpu.VMEM((n, rank_top, loads), F32),
            pltpu.VMEM((n // group, rows_here, group * rank_top), BF16),
            pltpu.VMEM((n // group, rows_here, group * rank_top), BF16),
            dma((7 + n // group,)),
            dma((2,)),
            dma((2,)),
            dma((2,)),
            dma((1,)),
            dma((n // group,)),
            pltpu.SemaphoreType.REGULAR((2,)),
        ],
        compiler_params=pltpu.CompilerParams(collective_id=0, has_side_effects=True),
    )(iterate, schur, near_block, u_basis, v_basis, tile_rank, send_rows, send_count)
    residual = rhs - applied
    updated = iterate + precond[:, None] * residual
    return (updated, residual)


def solution(mesh):
    in_specs = (
        P(("groups", "wide"), None),
        P(("groups", "wide"), None),
        P(("groups", "wide"), None, None),
        P(("groups", "wide"), None),
        P("groups", None, "wide"),
        P("groups", None, "wide"),
        P("groups", "wide"),
        P(("groups", "wide"), None, None),
        P(("groups", "wide"), None),
        P(("groups", "wide")),
    )
    out_specs = (P(("groups", "wide"), None), P(("groups", "wide"), None))
    return jax.shard_map(body, mesh=mesh, in_specs=in_specs, out_specs=out_specs, check_vma=False)
```

```python
import functools
import math

import jax
import jax.numpy as jnp
from jax import lax
from jax.experimental import pallas as pl
from jax.experimental.pallas import tpu as pltpu
from jax.sharding import PartitionSpec as P

MESH = pl.DeviceIdType.MESH
F32 = jnp.float32
BF16 = jnp.bfloat16

ALL, NEAR, FAR = 0, 1, 2
PLANS = [
    {0: [(0, NEAR)], 1: [(0, ALL)], 2: [(0, ALL)], 3: [(0, ALL)]},
    {0: [(1, ALL)], 1: [(1, ALL)], 3: [(1, ALL)]},
    {0: [(2, ALL), (0, FAR)], 3: [(2, ALL), (3, ALL)]},
    {2: [(1, ALL)]},
    {0: [(3, ALL)], 1: [(3, ALL), (2, ALL)], 2: [(3, ALL), (2, ALL)]},
]


def halves(x):
    high = x.astype(BF16)
    low = (x - high.astype(F32)).astype(BF16)
    return high, low


def mm(a, b):
    return jnp.dot(a, b, preferred_element_type=F32)


def pair(x):
    high, low = halves(x)
    return jnp.concatenate([high, low], axis=1), high


def fold(p):
    width = p.shape[1] // 2
    return p[:, :width] + p[:, width:]


def product(a_high, a_low, b_both, b_high):
    return fold(mm(a_high, b_both)) + mm(a_low, b_high)


def kernel(
    n,
    iterate_hbm, schur_hbm, near_hbm, u_hbm, v_hbm, rank_hbm, rows_hbm, count_hbm,
    out_ref,
    iterate, schur, near, u, v, rank, rows, count,
    edge_out, in_face, in_force, sent, gathered, u_high, u_low,
    load_sem, edge_send, face_recv, force_recv, send_sem, recv_sem, late_sem,
):
    me = lax.axis_index("wide")
    loads = iterate.shape[1]
    face = rows.shape[2]
    rank_top = v.shape[1]
    rows_here = iterate.shape[0]

    blocks = 4 if n % 4 == 0 else 1
    per_block = n // blocks
    group = math.gcd(per_block, max(1, 128 // rank_top))
    chunks = per_block // group
    block = lax.div(me, per_block)
    mine = lax.div(me, group)
    place_in_block = lax.rem(me, per_block)
    place_in_group = lax.rem(me, group)

    def by_block(first, second, third, fourth):
        at_least = [lax.div(block + 2, 3), lax.div(block, 2), lax.div(block, 3)]
        return first + (second - first) * at_least[0] + (third - second) * at_least[1] + (fourth - third) * at_least[2]

    if blocks == 4:
        send_order = [by_block(1, 2, 0, 0), by_block(0, 0, 1, 1), by_block(2, 1, 2, 2), 3]
        own_slot = by_block(1, 2, 2, 3)
        recv_order = [block, by_block(1, 0, 1, 2), by_block(3, 2, 0, 1), by_block(2, 3, 3, 0)]
    else:
        send_order, own_slot, recv_order = [0], 0, [0]

    def load(at, source, target):
        copy = pltpu.make_async_copy(source, target, load_sem.at[at])
        copy.start()
        return copy

    def load_v(slot, c):
        first = send_order[slot] * per_block + c * group
        at = slot * chunks + c
        return load(7 + at, v_hbm.at[pl.ds(first, group)], v.at[pl.ds(at * group, group)])

    iterate_load = load(0, iterate_hbm, iterate)
    barrier = pltpu.get_barrier_semaphore()

    def tell(semaphore, target):
        pl.semaphore_signal(semaphore, inc=1, device_id={"wide": target}, device_id_type=MESH)

    def tell_block(semaphore, target_block):
        for k in range(per_block):
            tell(semaphore, target_block * per_block + lax.rem(place_in_block + k, per_block))

    for k in range(1, per_block):
        tell(barrier, block * per_block + lax.rem(place_in_block + k, per_block))
    if blocks == 4:
        for target in range(blocks):
            last = [1, 2, 2, 3][target]

            @pl.when(jnp.logical_and(block != target, block <= last))
            def _():
                tell_block(barrier, target)

    def enter():
        pl.semaphore_wait(barrier, (per_block * by_block(2, 3, 3, 4) if blocks == 4 else n) - 1)

    def announce():
        if blocks == 4:
            @pl.when(block == 2)
            def _():
                tell_block(late_sem.at[0], 0)

            @pl.when(block == 3)
            def _():
                for target in range(3):
                    tell_block(late_sem.at[1], target)

    def late(which):
        if blocks == 4:
            @pl.when(block == 0 if which == 0 else block < 3)
            def _():
                pl.semaphore_wait(late_sem.at[which], per_block)

    rows_load = load(2, rows_hbm, rows)
    count_load = load(3, count_hbm, count)
    rank_load = load(1, rank_hbm, rank)
    v_loads = {(slot, c): load_v(slot, c) for slot in range(blocks) for c in range(chunks)}
    near_load = load(6, near_hbm, near)
    u_load = load(5, u_hbm, u)
    schur_load = load(4, schur_hbm, schur)

    @pl.when(me == 0)
    def _():
        in_face[2] = jnp.zeros_like(in_face[2])
        in_force[0] = jnp.zeros_like(in_force[0])

    @pl.when(me == n - 1)
    def _():
        in_face[0] = jnp.zeros_like(in_face[0])
        in_force[2] = jnp.zeros_like(in_force[2])

    below, above = lax.rem(me + n - 1, n), lax.rem(me + 1, n)
    has_below, has_above = me > 0, me < n - 1

    def edge_copy(side, kind, target, recv):
        return pltpu.make_async_remote_copy(
            src_ref=edge_out.at[side, kind], dst_ref=target, send_sem=edge_send.at[side], recv_sem=recv,
            device_id={"wide": above if side else below}, device_id_type=MESH,
        )

    face_down = edge_copy(0, 0, in_face.at[0], face_recv.at[0])
    face_up = edge_copy(1, 0, in_face.at[2], face_recv.at[1])
    force_up = edge_copy(1, 1, in_force.at[0], force_recv.at[0])
    force_down = edge_copy(0, 1, in_force.at[2], force_recv.at[1])

    iterate_load.wait()
    it_both, it_high = pair(iterate[...])
    rows_load.wait()
    count_load.wait()
    slot_ids = lax.broadcasted_iota(jnp.int32, (1, face), 1)
    row_of = [jnp.where(slot_ids < count[0, o], rows[o], -1) for o in range(3)]
    lanes = lax.broadcasted_iota(jnp.int32, (face, rows_here), 1)

    def picked(o):
        column = jnp.broadcast_to(row_of[o].astype(F32), (face, face)).T[:, :1].astype(jnp.int32)
        select = (column == lanes).astype(F32).astype(BF16)
        return fold(mm(select, it_both))

    edge_out[0, 0] = picked(0)
    edge_out[1, 0] = picked(2)

    rank_ids = lax.broadcasted_iota(jnp.int32, (rank_top, loads), 0)

    def compress(slot, c):
        v_loads[slot, c].wait()
        at = (slot * chunks + c) * group
        first = send_order[slot] * per_block + c * group
        v_high, v_low = halves(v[at : at + group].reshape(group * rank_top, rows_here))
        coeff = product(v_high, v_low, it_both, it_high)
        for g in range(group):
            part = coeff[g * rank_top : (g + 1) * rank_top]
            sent[at + g] = jnp.where(rank_ids < rank[0, first + g], part, 0.0)

    paired = group & (group - 1) == 0 and group > 1
    half = group // 2

    def flipped(k):
        moved = place_in_group
        for bit in [1 << b for b in range(group.bit_length()) if k >> b & 1]:
            moved = moved + bit * (1 - 2 * lax.rem(lax.div(place_in_group, bit), 2))
        return moved

    def member(k):
        if not paired:
            return lax.rem(place_in_group + k, group)
        k = int(bin(group + k)[:2:-1], 2)
        core = lax.rem(me, 2)
        return flipped(k) + core * (flipped(k ^ half) - flipped(k))

    def start(slot, c, in_group, may_be_me):
        target = send_order[slot] * per_block + c * group + in_group

        def go():
            pltpu.make_async_remote_copy(
                src_ref=sent.at[(slot * chunks + c) * group + in_group], dst_ref=gathered.at[me],
                send_sem=send_sem.at[0], recv_sem=recv_sem.at[mine],
                device_id={"wide": target}, device_id_type=MESH,
            ).start()

        if may_be_me:
            pl.when(target != me)(go)
        else:
            go()

    def send(stage):
        if blocks == 1:
            if stage == 2:
                for c in range(chunks):
                    for k in range(group):
                        start(0, c, member(k), True)
            return
        for b, plan in PLANS[stage].items():
            @pl.when(block == b)
            def _():
                for slot, part in plan:
                    own = slot == [1, 2, 2, 3][b]
                    for c in range(chunks):
                        if part == ALL or not paired:
                            if part == FAR:
                                continue
                            for k in range(group):
                                start(slot, c, member(k), own)
                        else:
                            for k in range(half) if part == NEAR else range(half, group):
                                start(slot, c, flipped(k), own and (k == 0 or chunks > 1))

    rank_load.wait()
    steps = [(slot, c) for slot in range(blocks) for c in range(chunks)]

    compress(*steps[0])
    enter()
    announce()
    waits_above = me == 3 * per_block - 1 if blocks == 4 else me < 0

    @pl.when(has_below)
    def _():
        face_down.start()

    @pl.when(jnp.logical_and(has_above, jnp.logical_not(waits_above)))
    def _():
        face_up.start()

    for step in steps[1:chunks]:
        compress(*step)
    send(0)
    for step in steps[chunks : 2 * chunks]:
        compress(*step)
    send(1)
    for step in steps[2 * chunks :]:
        compress(*step)
    gathered[me] = sent[own_slot * per_block + place_in_block]
    late(0)
    send(2)

    in_face[1] = picked(1)
    near_load.wait()
    near_high, near_low = halves(near[...])
    out_ref[...] = product(near_high, near_low, it_both, it_high)
    u_load.wait()
    for at in range(n // group):
        high, low = halves(u[at * group : (at + 1) * group].reshape(group * rank_top, rows_here).T)
        u_high[at] = high
        u_low[at] = low

    send(3)
    schur_load.wait()
    s_high, s_low = halves(schur[0])

    def force_part(o):
        span = slice(o * face, (o + 1) * face)
        b_both, b_high = pair(in_face[o])
        return product(s_high[:, span], s_low[:, span], b_both, b_high)

    force = force_part(1)
    late(1)

    @pl.when(waits_above)
    def _():
        face_up.start()

    send(4)

    def face_wait():
        @pl.when(has_above)
        def _():
            face_down.wait_recv()

        @pl.when(has_below)
        def _():
            face_up.wait_recv()

    face_wait()
    force = force + force_part(0) + force_part(2)
    edge_out[0, 1] = force[2 * face :]
    edge_out[1, 1] = force[:face]
    in_force[1] = force[face : 2 * face]

    @pl.when(has_above)
    def _():
        force_up.start()

    @pl.when(has_below)
    def _():
        force_down.start()

    place = lax.broadcasted_iota(jnp.int32, (rows_here, face), 0)

    def scattered(o):
        scatter = (place == row_of[o]).astype(F32).astype(BF16)
        b_both, _ = pair(in_force[o])
        return fold(mm(scatter, b_both))

    def far_wait(slot, c):
        at = recv_order[slot] * chunks + c

        def arrived(tiles):
            span = gathered.at[pl.ds(0, tiles)]
            pltpu.make_async_remote_copy(
                src_ref=span, dst_ref=span, send_sem=send_sem.at[0], recv_sem=recv_sem.at[at],
                device_id={"wide": above}, device_id_type=MESH,
            ).wait_recv()

        def wait():
            if slot > 0:
                arrived(group)
                return
            if group > 1:
                @pl.when(at == mine)
                def _():
                    arrived(group - 1)

            if chunks > 1:
                @pl.when(at != mine)
                def _():
                    arrived(group)

        wait()

    def far(slot, c):
        at = recv_order[slot] * chunks + c
        got = gathered[pl.ds(at * group, group)].reshape(group * rank_top, loads)
        b_both, b_high = pair(got)
        return product(u_high[at], u_low[at], b_both, b_high)

    out_ref[...] += scattered(1)
    order = [(slot, c) for slot in range(blocks) for c in range(chunks)]
    for step in order[:-1]:
        far_wait(*step)
        out_ref[...] += far(*step)

    def force_wait():
        @pl.when(has_below)
        def _():
            force_up.wait_recv()

        @pl.when(has_above)
        def _():
            force_down.wait_recv()

    far_wait(*order[-1])
    force_wait()
    out_ref[...] += far(*order[-1]) + (scattered(0) + scattered(2))

    def sent_wait():
        @pl.when(has_below)
        def _():
            pltpu.make_async_remote_copy(
                src_ref=edge_out.at[0], dst_ref=edge_out.at[0], send_sem=edge_send.at[0],
                recv_sem=face_recv.at[0], device_id={"wide": below}, device_id_type=MESH,
            ).wait_send()

        @pl.when(has_above)
        def _():
            pltpu.make_async_remote_copy(
                src_ref=edge_out.at[1], dst_ref=edge_out.at[1], send_sem=edge_send.at[1],
                recv_sem=face_recv.at[1], device_id={"wide": above}, device_id_type=MESH,
            ).wait_send()

        all_sent = sent.at[pl.ds(0, n - 1)]
        pltpu.make_async_remote_copy(
            src_ref=all_sent, dst_ref=all_sent, send_sem=send_sem.at[0], recv_sem=recv_sem.at[0],
            device_id={"wide": above}, device_id_type=MESH,
        ).wait_send()

    sent_wait()


def body(
    iterate, rhs, schur, near_block, u_basis, v_basis, tile_rank, send_rows, send_count, precond
):
    n = lax.axis_size("wide")
    rows_here, loads = iterate.shape
    face = send_rows.shape[2]
    tiles, rank_top, _ = u_basis.shape
    group = math.gcd(n // 4 if n % 4 == 0 else n, max(1, 128 // rank_top))
    tile_rank = tile_rank.reshape(1, tiles)
    send_rows = send_rows.reshape(3, 1, face)
    dma = pltpu.SemaphoreType.DMA
    applied = pl.pallas_call(
        functools.partial(kernel, n),
        out_shape=pltpu.VMEM((rows_here, loads), F32),
        in_specs=[pl.BlockSpec(memory_space=pl.ANY)] * 8,
        out_specs=pl.BlockSpec(memory_space=pltpu.VMEM),
        scratch_shapes=[
            pltpu.VMEM(iterate.shape, F32),
            pltpu.VMEM(schur.shape, F32),
            pltpu.VMEM(near_block.shape, F32),
            pltpu.VMEM(u_basis.shape, F32),
            pltpu.VMEM(v_basis.shape, F32),
            pltpu.SMEM(tile_rank.shape, jnp.int32),
            pltpu.VMEM(send_rows.shape, jnp.int32),
            pltpu.SMEM(send_count.shape, jnp.int32),
            pltpu.VMEM((2, 2, face, loads), F32),
            pltpu.VMEM((3, face, loads), F32),
            pltpu.VMEM((3, face, loads), F32),
            pltpu.VMEM((n, rank_top, loads), F32),
            pltpu.VMEM((n, rank_top, loads), F32),
            pltpu.VMEM((n // group, rows_here, group * rank_top), BF16),
            pltpu.VMEM((n // group, rows_here, group * rank_top), BF16),
            dma((7 + n // group,)),
            dma((2,)),
            dma((2,)),
            dma((2,)),
            dma((1,)),
            dma((n // group,)),
            pltpu.SemaphoreType.REGULAR((2,)),
        ],
        compiler_params=pltpu.CompilerParams(collective_id=0, has_side_effects=True),
    )(iterate, schur, near_block, u_basis, v_basis, tile_rank, send_rows, send_count)
    residual = rhs - applied
    updated = iterate + precond[:, None] * residual
    return (updated, residual)


def solution(mesh):
    in_specs = (
        P(("groups", "wide"), None),
        P(("groups", "wide"), None),
        P(("groups", "wide"), None, None),
        P(("groups", "wide"), None),
        P("groups", None, "wide"),
        P("groups", None, "wide"),
        P("groups", "wide"),
        P(("groups", "wide"), None, None),
        P(("groups", "wide"), None),
        P(("groups", "wide")),
    )
    out_specs = (P(("groups", "wide"), None), P(("groups", "wide"), None))
    return jax.shard_map(body, mesh=mesh, in_specs=in_specs, out_specs=out_specs, check_vma=False)
```

```python
import functools
import math

import jax
import jax.numpy as jnp
from jax import lax
from jax.experimental import pallas as pl
from jax.experimental.pallas import tpu as pltpu
from jax.sharding import PartitionSpec as P

MESH = pl.DeviceIdType.MESH
F32 = jnp.float32
BF16 = jnp.bfloat16

ALL, NEAR, FAR = 0, 1, 2
EACH, FIRST, REST, LOW, HIGH = range(5)
PLANS = [
    {0: [(0, NEAR, EACH)], 1: [(0, ALL, FIRST), (0, ALL, REST)], 2: [(0, ALL, EACH)], 3: [(0, ALL, EACH)]},
    {0: [(1, ALL, EACH)], 1: [(1, ALL, REST)]},
    {0: [(2, ALL, EACH), (0, FAR, EACH)], 1: [(1, ALL, FIRST)], 3: [(2, ALL, EACH), (3, ALL, EACH)]},
    {2: [(1, ALL, EACH)], 3: [(1, ALL, EACH)]},
    {0: [(3, ALL, EACH)], 1: [(3, ALL, LOW), (3, FAR, HIGH), (2, ALL, EACH)], 2: [(3, ALL, EACH), (2, ALL, EACH)]},
    {1: [(3, NEAR, HIGH)]},
]


def halves(x):
    high = x.astype(BF16)
    low = (x - high.astype(F32)).astype(BF16)
    return high, low


def mm(a, b):
    return jnp.dot(a, b, preferred_element_type=F32)


def pair(x):
    high, low = halves(x)
    return jnp.concatenate([high, low], axis=1), high


def fold(p):
    width = p.shape[1] // 2
    return p[:, :width] + p[:, width:]


def product(a_high, a_low, b_both, b_high):
    return fold(mm(a_high, b_both)) + mm(a_low, b_high)


def kernel(
    n,
    iterate_hbm, schur_hbm, near_hbm, u_hbm, v_hbm, rank_hbm, rows_hbm, count_hbm,
    out_ref,
    iterate, schur, near, u, v, rank, rows, count,
    edge_out, in_face, in_force, sent, gathered, u_high, u_low,
    load_sem, edge_send, face_recv, force_recv, send_sem, recv_sem, late_sem,
):
    me = lax.axis_index("wide")
    loads = iterate.shape[1]
    face = rows.shape[2]
    rank_top = v.shape[1]
    rows_here = iterate.shape[0]

    blocks = 4 if n % 4 == 0 else 1
    per_block = n // blocks
    group = math.gcd(per_block, max(1, 128 // rank_top))
    chunks = per_block // group
    block = lax.div(me, per_block)
    mine = lax.div(me, group)
    place_in_block = lax.rem(me, per_block)
    place_in_group = lax.rem(me, group)

    def by_block(first, second, third, fourth):
        at_least = [lax.div(block + 2, 3), lax.div(block, 2), lax.div(block, 3)]
        return first + (second - first) * at_least[0] + (third - second) * at_least[1] + (fourth - third) * at_least[2]

    if blocks == 4:
        upper = lax.div(place_in_block + per_block - 1, per_block)
        send_order = [by_block(1, 2 * upper, 0, 0), by_block(0, 2 - 2 * upper, 1, 1), by_block(2, 1, 2, 2), 3]
        own_slot = by_block(1, 2, 2, 3)
        recv_order = [block, by_block(1, 0, 1, 2), by_block(3, 2, 0, 1), by_block(2, 3, 3, 0)]
    else:
        send_order, own_slot, recv_order = [0], 0, [0]

    def load(at, source, target):
        copy = pltpu.make_async_copy(source, target, load_sem.at[at])
        copy.start()
        return copy

    def load_v(slot, c):
        first = send_order[slot] * per_block + c * group
        at = slot * chunks + c
        return load(7 + at, v_hbm.at[pl.ds(first, group)], v.at[pl.ds(at * group, group)])

    rows_load = load(2, rows_hbm, rows)
    count_load = load(3, count_hbm, count)
    quarter = rows_here // 4
    for part in range(4):
        span = pl.ds(part * quarter, quarter)
        pltpu.make_async_copy(iterate_hbm.at[span], iterate.at[span], load_sem.at[0]).start()
    iterate_load = pltpu.make_async_copy(iterate_hbm, iterate, load_sem.at[0])
    barrier = pltpu.get_barrier_semaphore()

    def tell(semaphore, target):
        pl.semaphore_signal(semaphore, inc=1, device_id={"wide": target}, device_id_type=MESH)

    def tell_block(semaphore, target_block):
        for k in range(per_block):
            tell(semaphore, target_block * per_block + lax.rem(place_in_block + k, per_block))

    def tell_rest(semaphore, target_block):
        rest = per_block - 1
        for k in range(rest):
            tell(semaphore, target_block * per_block + 1 + lax.rem(place_in_block + k, rest))

    for k in range(1, per_block):
        tell(barrier, block * per_block + lax.rem(place_in_block + k, per_block))
    if blocks == 4:
        for target in range(blocks):
            last = [1, 1, 2, 3][target]

            @pl.when(jnp.logical_and(block != target, block <= last))
            def _():
                tell_block(barrier, target)

        @pl.when(block == 2)
        def _():
            tell_rest(barrier, 1)

    def enter():
        pl.semaphore_wait(barrier, (per_block * by_block(2, 2 + upper, 3, 4) if blocks == 4 else n) - 1)

    def announce():
        if blocks == 4:
            @pl.when(block == 2)
            def _():
                tell_block(late_sem.at[0], 0)
                tell(late_sem.at[0], per_block)

            @pl.when(block == 3)
            def _():
                for target in range(3):
                    tell_block(late_sem.at[1], target)

    def late(which):
        if blocks == 4:
            @pl.when(me < per_block + 1 if which == 0 else block < 3)
            def _():
                pl.semaphore_wait(late_sem.at[which], per_block)

    rank_load = load(1, rank_hbm, rank)
    v_loads = {(slot, c): load_v(slot, c) for slot in range(blocks) for c in range(chunks)}
    near_load = load(6, near_hbm, near)
    u_load = load(5, u_hbm, u)
    schur_load = load(4, schur_hbm, schur)

    @pl.when(me == 0)
    def _():
        in_face[2] = jnp.zeros_like(in_face[2])
        in_force[0] = jnp.zeros_like(in_force[0])

    @pl.when(me == n - 1)
    def _():
        in_face[0] = jnp.zeros_like(in_face[0])
        in_force[2] = jnp.zeros_like(in_force[2])

    below, above = lax.rem(me + n - 1, n), lax.rem(me + 1, n)
    has_below, has_above = me > 0, me < n - 1

    def edge_copy(side, kind, target, recv):
        return pltpu.make_async_remote_copy(
            src_ref=edge_out.at[side, kind], dst_ref=target, send_sem=edge_send.at[side], recv_sem=recv,
            device_id={"wide": above if side else below}, device_id_type=MESH,
        )

    face_down = edge_copy(0, 0, in_face.at[0], face_recv.at[0])
    face_up = edge_copy(1, 0, in_face.at[2], face_recv.at[1])
    force_up = edge_copy(1, 1, in_force.at[0], force_recv.at[0])
    force_down = edge_copy(0, 1, in_force.at[2], force_recv.at[1])

    rows_load.wait()
    count_load.wait()
    slot_ids = lax.broadcasted_iota(jnp.int32, (1, face), 1)
    row_of = [jnp.where(slot_ids < count[0, o], rows[o], -1) for o in range(3)]
    lanes = lax.broadcasted_iota(jnp.int32, (face, rows_here), 1)

    def selection(o):
        column = jnp.broadcast_to(row_of[o].astype(F32), (face, face)).T[:, :1].astype(jnp.int32)
        return (column == lanes).astype(F32).astype(BF16)

    selections = [selection(0), None, selection(2)]
    iterate_load.wait()
    it_both, it_high = pair(iterate[...])

    def picked(o):
        select = selection(o) if selections[o] is None else selections[o]
        return fold(mm(select, it_both))

    edge_out[0, 0] = picked(0)
    edge_out[1, 0] = picked(2)

    rank_ids = lax.broadcasted_iota(jnp.int32, (rank_top, loads), 0)

    def compress(slot, c):
        v_loads[slot, c].wait()
        at = (slot * chunks + c) * group
        first = send_order[slot] * per_block + c * group
        v_high, v_low = halves(v[at : at + group].reshape(group * rank_top, rows_here))
        coeff = product(v_high, v_low, it_both, it_high)
        for g in range(group):
            part = coeff[g * rank_top : (g + 1) * rank_top]
            sent[at + g] = jnp.where(rank_ids < rank[0, first + g], part, 0.0)

    paired = group & (group - 1) == 0 and group > 1
    half = group // 2

    def flipped(k):
        moved = place_in_group
        for bit in [1 << b for b in range(group.bit_length()) if k >> b & 1]:
            moved = moved + bit * (1 - 2 * lax.rem(lax.div(place_in_group, bit), 2))
        return moved

    def member(k):
        if not paired:
            return lax.rem(place_in_group + k, group)
        k = int(bin(group + k)[:2:-1], 2)
        core = lax.rem(me, 2)
        return flipped(k) + core * (flipped(k ^ half) - flipped(k))

    def start(slot, c, in_group, may_be_me):
        target = send_order[slot] * per_block + c * group + in_group

        def go():
            pltpu.make_async_remote_copy(
                src_ref=sent.at[(slot * chunks + c) * group + in_group], dst_ref=gathered.at[me],
                send_sem=send_sem.at[0], recv_sem=recv_sem.at[mine],
                device_id={"wide": target}, device_id_type=MESH,
            ).start()

        if may_be_me:
            pl.when(target != me)(go)
        else:
            go()

    def send_slot(b, slot, part):
        own = slot == [1, 2, 2, 3][b]
        for c in range(chunks):
            if part == ALL or not paired:
                if part == FAR:
                    continue
                for k in range(group):
                    start(slot, c, member(k), own)
            else:
                for k in range(half) if part == NEAR else range(half, group):
                    start(slot, c, flipped(k), own and (k == 0 or chunks > 1))

    def send(stage):
        if blocks == 1:
            if stage == 2:
                for c in range(chunks):
                    for k in range(group):
                        start(0, c, member(k), True)
            return
        for b, plan in PLANS[stage].items():
            @pl.when(block == b)
            def _():
                for slot, part, who in plan:
                    if who == EACH:
                        send_slot(b, slot, part)
                    else:
                        high = lax.div(place_in_block, per_block // 2)
                        chosen = {FIRST: upper == 0, REST: upper == 1, LOW: high == 0, HIGH: high == 1}[who]
                        pl.when(chosen)(functools.partial(send_slot, b, slot, part))

    rank_load.wait()
    steps = [(slot, c) for slot in range(blocks) for c in range(chunks)]

    compress(*steps[0])
    enter()
    announce()
    waits_above = me == 3 * per_block - 1 if blocks == 4 else me < 0

    @pl.when(has_below)
    def _():
        face_down.start()

    @pl.when(jnp.logical_and(has_above, jnp.logical_not(waits_above)))
    def _():
        face_up.start()

    for step in steps[1:chunks]:
        compress(*step)
    send(0)
    for step in steps[chunks : 2 * chunks]:
        compress(*step)
    send(1)
    for step in steps[2 * chunks :]:
        compress(*step)
    gathered[me] = sent[own_slot * per_block + place_in_block]
    late(0)
    send(2)

    in_face[1] = picked(1)
    near_load.wait()
    near_high, near_low = halves(near[...])
    out_ref[...] = product(near_high, near_low, it_both, it_high)
    u_load.wait()
    for at in range(n // group):
        high, low = halves(u[at * group : (at + 1) * group].reshape(group * rank_top, rows_here).T)
        u_high[at] = high
        u_low[at] = low

    send(3)
    schur_load.wait()
    s_high, s_low = halves(schur[0])

    def force_part(o):
        span = slice(o * face, (o + 1) * face)
        b_both, b_high = pair(in_face[o])
        return product(s_high[:, span], s_low[:, span], b_both, b_high)

    force = force_part(1)
    late(1)

    @pl.when(waits_above)
    def _():
        face_up.start()

    send(4)

    def face_wait():
        @pl.when(has_above)
        def _():
            face_down.wait_recv()

        @pl.when(has_below)
        def _():
            face_up.wait_recv()

    face_wait()
    force = force + force_part(0) + force_part(2)
    edge_out[0, 1] = force[2 * face :]
    edge_out[1, 1] = force[:face]
    in_force[1] = force[face : 2 * face]

    @pl.when(has_above)
    def _():
        force_up.start()

    @pl.when(has_below)
    def _():
        force_down.start()

    send(5)
    place = lax.broadcasted_iota(jnp.int32, (rows_here, face), 0)

    def scattered(o):
        scatter = (place == row_of[o]).astype(F32).astype(BF16)
        b_both, _ = pair(in_force[o])
        return fold(mm(scatter, b_both))

    def far_wait(slot, c):
        at = recv_order[slot] * chunks + c

        def arrived(tiles):
            span = gathered.at[pl.ds(0, tiles)]
            pltpu.make_async_remote_copy(
                src_ref=span, dst_ref=span, send_sem=send_sem.at[0], recv_sem=recv_sem.at[at],
                device_id={"wide": above}, device_id_type=MESH,
            ).wait_recv()

        def wait():
            if slot > 0:
                arrived(group)
                return
            if group > 1:
                @pl.when(at == mine)
                def _():
                    arrived(group - 1)

            if chunks > 1:
                @pl.when(at != mine)
                def _():
                    arrived(group)

        wait()

    def far(slot, c):
        at = recv_order[slot] * chunks + c
        got = gathered[pl.ds(at * group, group)].reshape(group * rank_top, loads)
        b_both, b_high = pair(got)
        return product(u_high[at], u_low[at], b_both, b_high)

    out_ref[...] += scattered(1)
    order = [(slot, c) for slot in range(blocks) for c in range(chunks)]
    for step in order[:-1]:
        far_wait(*step)
        out_ref[...] += far(*step)

    def force_wait():
        @pl.when(has_below)
        def _():
            force_up.wait_recv()

        @pl.when(has_above)
        def _():
            force_down.wait_recv()

    far_wait(*order[-1])
    force_wait()
    out_ref[...] += far(*order[-1]) + (scattered(0) + scattered(2))

    def sent_wait():
        @pl.when(has_below)
        def _():
            pltpu.make_async_remote_copy(
                src_ref=edge_out.at[0], dst_ref=edge_out.at[0], send_sem=edge_send.at[0],
                recv_sem=face_recv.at[0], device_id={"wide": below}, device_id_type=MESH,
            ).wait_send()

        @pl.when(has_above)
        def _():
            pltpu.make_async_remote_copy(
                src_ref=edge_out.at[1], dst_ref=edge_out.at[1], send_sem=edge_send.at[1],
                recv_sem=face_recv.at[1], device_id={"wide": above}, device_id_type=MESH,
            ).wait_send()

        all_sent = sent.at[pl.ds(0, n - 1)]
        pltpu.make_async_remote_copy(
            src_ref=all_sent, dst_ref=all_sent, send_sem=send_sem.at[0], recv_sem=recv_sem.at[0],
            device_id={"wide": above}, device_id_type=MESH,
        ).wait_send()

    sent_wait()


def body(
    iterate, rhs, schur, near_block, u_basis, v_basis, tile_rank, send_rows, send_count, precond
):
    n = lax.axis_size("wide")
    rows_here, loads = iterate.shape
    face = send_rows.shape[2]
    tiles, rank_top, _ = u_basis.shape
    group = math.gcd(n // 4 if n % 4 == 0 else n, max(1, 128 // rank_top))
    tile_rank = tile_rank.reshape(1, tiles)
    send_rows = send_rows.reshape(3, 1, face)
    dma = pltpu.SemaphoreType.DMA
    applied = pl.pallas_call(
        functools.partial(kernel, n),
        out_shape=pltpu.VMEM((rows_here, loads), F32),
        in_specs=[pl.BlockSpec(memory_space=pl.ANY)] * 8,
        out_specs=pl.BlockSpec(memory_space=pltpu.VMEM),
        scratch_shapes=[
            pltpu.VMEM(iterate.shape, F32),
            pltpu.VMEM(schur.shape, F32),
            pltpu.VMEM(near_block.shape, F32),
            pltpu.VMEM(u_basis.shape, F32),
            pltpu.VMEM(v_basis.shape, F32),
            pltpu.SMEM(tile_rank.shape, jnp.int32),
            pltpu.VMEM(send_rows.shape, jnp.int32),
            pltpu.SMEM(send_count.shape, jnp.int32),
            pltpu.VMEM((2, 2, face, loads), F32),
            pltpu.VMEM((3, face, loads), F32),
            pltpu.VMEM((3, face, loads), F32),
            pltpu.VMEM((n, rank_top, loads), F32),
            pltpu.VMEM((n, rank_top, loads), F32),
            pltpu.VMEM((n // group, rows_here, group * rank_top), BF16),
            pltpu.VMEM((n // group, rows_here, group * rank_top), BF16),
            dma((7 + n // group,)),
            dma((2,)),
            dma((2,)),
            dma((2,)),
            dma((1,)),
            dma((n // group,)),
            pltpu.SemaphoreType.REGULAR((2,)),
        ],
        compiler_params=pltpu.CompilerParams(collective_id=0, has_side_effects=True),
    )(iterate, schur, near_block, u_basis, v_basis, tile_rank, send_rows, send_count)
    residual = rhs - applied
    updated = iterate + precond[:, None] * residual
    return (updated, residual)


def solution(mesh):
    in_specs = (
        P(("groups", "wide"), None),
        P(("groups", "wide"), None),
        P(("groups", "wide"), None, None),
        P(("groups", "wide"), None),
        P("groups", None, "wide"),
        P("groups", None, "wide"),
        P("groups", "wide"),
        P(("groups", "wide"), None, None),
        P(("groups", "wide"), None),
        P(("groups", "wide")),
    )
    out_specs = (P(("groups", "wide"), None), P(("groups", "wide"), None))
    return jax.shard_map(body, mesh=mesh, in_specs=in_specs, out_specs=out_specs, check_vma=False)
```

```python
import functools
import math

import jax
import jax.numpy as jnp
from jax import lax
from jax.experimental import pallas as pl
from jax.experimental.pallas import tpu as pltpu
from jax.sharding import PartitionSpec as P

MESH = pl.DeviceIdType.MESH
F32 = jnp.float32
BF16 = jnp.bfloat16

ALL, NEAR, FAR = 0, 1, 2
EACH, FIRST, REST, LOW, HIGH = range(5)
PLANS = [
    {0: [(0, NEAR, EACH)], 1: [(0, ALL, FIRST), (0, ALL, REST)], 2: [(0, ALL, EACH)], 3: [(0, ALL, EACH)]},
    {0: [(1, ALL, EACH)], 1: [(1, ALL, REST)]},
    {0: [(2, ALL, EACH), (0, FAR, EACH)], 1: [(1, ALL, FIRST)], 3: [(2, ALL, EACH), (3, ALL, EACH)]},
    {1: [(2, ALL, HIGH)], 2: [(1, ALL, EACH)], 3: [(1, ALL, EACH)]},
    {0: [(3, ALL, EACH)], 1: [(3, ALL, LOW), (3, FAR, HIGH), (2, ALL, LOW)], 2: [(3, ALL, EACH), (2, ALL, EACH)]},
    {1: [(3, NEAR, HIGH)]},
]


def halves(x):
    high = x.astype(BF16)
    low = (x - high.astype(F32)).astype(BF16)
    return high, low


def mm(a, b):
    return jnp.dot(a, b, preferred_element_type=F32)


def pair(x):
    high, low = halves(x)
    return jnp.concatenate([high, low], axis=1), high


def fold(p):
    width = p.shape[1] // 2
    return p[:, :width] + p[:, width:]


def product(a_high, a_low, b_both, b_high):
    return fold(mm(a_high, b_both)) + mm(a_low, b_high)


def kernel(
    n,
    iterate_hbm, schur_hbm, near_hbm, u_hbm, v_hbm, rank_hbm, rows_hbm, count_hbm,
    out_ref,
    iterate, schur, near, u, v, rank, rows, count,
    edge_out, in_face, in_force, sent, gathered, u_high, u_low,
    load_sem, edge_send, face_recv, force_recv, send_sem, recv_sem, late_sem,
):
    me = lax.axis_index("wide")
    loads = iterate.shape[1]
    face = rows.shape[2]
    rank_top = v.shape[1]
    rows_here = iterate.shape[0]

    blocks = 4 if n % 4 == 0 else 1
    per_block = n // blocks
    group = math.gcd(per_block, max(1, 128 // rank_top))
    chunks = per_block // group
    block = lax.div(me, per_block)
    mine = lax.div(me, group)
    place_in_block = lax.rem(me, per_block)
    place_in_group = lax.rem(me, group)

    def by_block(first, second, third, fourth):
        at_least = [lax.div(block + 2, 3), lax.div(block, 2), lax.div(block, 3)]
        return first + (second - first) * at_least[0] + (third - second) * at_least[1] + (fourth - third) * at_least[2]

    if blocks == 4:
        upper = lax.div(place_in_block + per_block - 1, per_block)
        send_order = [by_block(1, 2 * upper, 0, 0), by_block(0, 2 - 2 * upper, 1, 1), by_block(2, 1, 2, 2), 3]
        own_slot = by_block(1, 2, 2, 3)
        recv_order = [block, by_block(1, 0, 1, 2), by_block(3, 2, 0, 1), by_block(2, 3, 3, 0)]
    else:
        send_order, own_slot, recv_order = [0], 0, [0]

    def load(at, source, target):
        copy = pltpu.make_async_copy(source, target, load_sem.at[at])
        copy.start()
        return copy

    def load_v(slot, c):
        first = send_order[slot] * per_block + c * group
        at = slot * chunks + c
        return load(3 + at, v_hbm.at[pl.ds(first, group)], v.at[pl.ds(at * group, group)])

    rows_load = load(1, rows_hbm, rows)
    count_load = load(1, count_hbm, count)
    quarter = rows_here // 4
    for part in range(4):
        span = pl.ds(part * quarter, quarter)
        pltpu.make_async_copy(iterate_hbm.at[span], iterate.at[span], load_sem.at[0]).start()
    iterate_load = pltpu.make_async_copy(iterate_hbm, iterate, load_sem.at[0])
    barrier = pltpu.get_barrier_semaphore()

    def tell(semaphore, target):
        pl.semaphore_signal(semaphore, inc=1, device_id={"wide": target}, device_id_type=MESH)

    def tell_block(semaphore, target_block):
        for k in range(per_block):
            tell(semaphore, target_block * per_block + lax.rem(place_in_block + k, per_block))

    def tell_rest(semaphore, target_block):
        rest = per_block - 1
        for k in range(rest):
            tell(semaphore, target_block * per_block + 1 + lax.rem(place_in_block + k, rest))

    for k in range(1, per_block):
        tell(barrier, block * per_block + lax.rem(place_in_block + k, per_block))
    if blocks == 4:
        for target in range(blocks):
            last = [1, 1, 2, 3][target]

            @pl.when(jnp.logical_and(block != target, block <= last))
            def _():
                tell_block(barrier, target)

        @pl.when(block == 2)
        def _():
            tell_rest(barrier, 1)

    def enter():
        pl.semaphore_wait(barrier, (per_block * by_block(2, 2 + upper, 3, 4) if blocks == 4 else n) - 1)

    def announce():
        if blocks == 4:
            @pl.when(block == 2)
            def _():
                tell_block(late_sem.at[0], 0)
                tell(late_sem.at[0], per_block)

            @pl.when(block == 3)
            def _():
                for target in range(3):
                    tell_block(late_sem.at[1], target)

    def late(which):
        if blocks == 4:
            @pl.when(me < per_block + 1 if which == 0 else block < 3)
            def _():
                pl.semaphore_wait(late_sem.at[which], per_block)

    rank_load = load(1, rank_hbm, rank)
    v_loads = {(slot, c): load_v(slot, c) for slot in range(blocks) for c in range(chunks)}
    near_load = load(2, near_hbm, near)
    u_load = load(2, u_hbm, u)
    schur_load = load(2, schur_hbm, schur)

    @pl.when(me == 0)
    def _():
        in_face[2] = jnp.zeros_like(in_face[2])
        in_force[0] = jnp.zeros_like(in_force[0])

    @pl.when(me == n - 1)
    def _():
        in_face[0] = jnp.zeros_like(in_face[0])
        in_force[2] = jnp.zeros_like(in_force[2])

    below, above = lax.rem(me + n - 1, n), lax.rem(me + 1, n)
    has_below, has_above = me > 0, me < n - 1

    def edge_copy(side, kind, target, recv):
        return pltpu.make_async_remote_copy(
            src_ref=edge_out.at[side, kind], dst_ref=target, send_sem=edge_send.at[side], recv_sem=recv,
            device_id={"wide": above if side else below}, device_id_type=MESH,
        )

    face_down = edge_copy(0, 0, in_face.at[0], face_recv.at[0])
    face_up = edge_copy(1, 0, in_face.at[2], face_recv.at[1])
    force_up = edge_copy(1, 1, in_force.at[0], force_recv.at[0])
    force_down = edge_copy(0, 1, in_force.at[2], force_recv.at[1])

    rows_load.wait()
    count_load.wait()
    rank_load.wait()
    slot_ids = lax.broadcasted_iota(jnp.int32, (1, face), 1)
    row_of = [jnp.where(slot_ids < count[0, o], rows[o], -1) for o in range(3)]
    lanes = lax.broadcasted_iota(jnp.int32, (face, rows_here), 1)

    def selection(o):
        column = jnp.broadcast_to(row_of[o].astype(F32), (face, face)).T[:, :1].astype(jnp.int32)
        return (column == lanes).astype(F32).astype(BF16)

    selections = [selection(0), None, selection(2)]
    iterate_load.wait()
    it_both, it_high = pair(iterate[...])

    def picked(o):
        select = selection(o) if selections[o] is None else selections[o]
        return fold(mm(select, it_both))

    edge_out[0, 0] = picked(0)
    edge_out[1, 0] = picked(2)

    rank_ids = lax.broadcasted_iota(jnp.int32, (rank_top, loads), 0)

    def compress(slot, c):
        v_loads[slot, c].wait()
        at = (slot * chunks + c) * group
        first = send_order[slot] * per_block + c * group
        v_high, v_low = halves(v[at : at + group].reshape(group * rank_top, rows_here))
        coeff = product(v_high, v_low, it_both, it_high)
        for g in range(group):
            part = coeff[g * rank_top : (g + 1) * rank_top]
            sent[at + g] = jnp.where(rank_ids < rank[0, first + g], part, 0.0)

    paired = group & (group - 1) == 0 and group > 1
    half = group // 2

    def flipped(k):
        moved = place_in_group
        for bit in [1 << b for b in range(group.bit_length()) if k >> b & 1]:
            moved = moved + bit * (1 - 2 * lax.rem(lax.div(place_in_group, bit), 2))
        return moved

    def member(k):
        if not paired:
            return lax.rem(place_in_group + k, group)
        k = int(bin(group + k)[:2:-1], 2)
        core = lax.rem(me, 2)
        return flipped(k) + core * (flipped(k ^ half) - flipped(k))

    def start(slot, c, in_group, may_be_me):
        target = send_order[slot] * per_block + c * group + in_group

        def go():
            pltpu.make_async_remote_copy(
                src_ref=sent.at[(slot * chunks + c) * group + in_group], dst_ref=gathered.at[me],
                send_sem=send_sem.at[0], recv_sem=recv_sem.at[mine],
                device_id={"wide": target}, device_id_type=MESH,
            ).start()

        if may_be_me:
            pl.when(target != me)(go)
        else:
            go()

    def send_slot(b, slot, part):
        own = slot == [1, 2, 2, 3][b]
        for c in range(chunks):
            if part == ALL or not paired:
                if part == FAR:
                    continue
                for k in range(group):
                    start(slot, c, member(k), own)
            else:
                for k in range(half) if part == NEAR else range(half, group):
                    start(slot, c, flipped(k), own and (k == 0 or chunks > 1))

    def send(stage):
        if blocks == 1:
            if stage == 2:
                for c in range(chunks):
                    for k in range(group):
                        start(0, c, member(k), True)
            return
        for b, plan in PLANS[stage].items():
            @pl.when(block == b)
            def _():
                for slot, part, who in plan:
                    if who == EACH:
                        send_slot(b, slot, part)
                    else:
                        high = lax.div(place_in_block, per_block // 2)
                        chosen = {FIRST: upper == 0, REST: upper == 1, LOW: high == 0, HIGH: high == 1}[who]
                        pl.when(chosen)(functools.partial(send_slot, b, slot, part))

    steps = [(slot, c) for slot in range(blocks) for c in range(chunks)]

    compress(*steps[0])
    enter()
    announce()
    waits_above = me == 3 * per_block - 1 if blocks == 4 else me < 0

    @pl.when(has_below)
    def _():
        face_down.start()

    @pl.when(jnp.logical_and(has_above, jnp.logical_not(waits_above)))
    def _():
        face_up.start()

    for step in steps[1:chunks]:
        compress(*step)
    send(0)
    for step in steps[chunks : 2 * chunks]:
        compress(*step)
    send(1)
    for step in steps[2 * chunks :]:
        compress(*step)
    gathered[me] = sent[own_slot * per_block + place_in_block]
    late(0)
    send(2)

    in_face[1] = picked(1)
    near_load.wait()
    u_load.wait()
    schur_load.wait()
    near_high, near_low = halves(near[...])
    out_ref[...] = product(near_high, near_low, it_both, it_high)
    for at in range(n // group):
        high, low = halves(u[at * group : (at + 1) * group].reshape(group * rank_top, rows_here).T)
        u_high[at] = high
        u_low[at] = low

    send(3)
    s_high, s_low = halves(schur[0])

    def force_part(o):
        span = slice(o * face, (o + 1) * face)
        b_both, b_high = pair(in_face[o])
        return product(s_high[:, span], s_low[:, span], b_both, b_high)

    force = force_part(1)
    late(1)

    @pl.when(waits_above)
    def _():
        face_up.start()

    send(4)

    def face_wait():
        @pl.when(has_above)
        def _():
            face_down.wait_recv()

        @pl.when(has_below)
        def _():
            face_up.wait_recv()

    face_wait()
    force = force + force_part(0) + force_part(2)
    edge_out[0, 1] = force[2 * face :]
    edge_out[1, 1] = force[:face]
    in_force[1] = force[face : 2 * face]

    @pl.when(has_above)
    def _():
        force_up.start()

    @pl.when(has_below)
    def _():
        force_down.start()

    send(5)
    place = lax.broadcasted_iota(jnp.int32, (rows_here, face), 0)

    def scattered(o):
        scatter = (place == row_of[o]).astype(F32).astype(BF16)
        b_both, _ = pair(in_force[o])
        return fold(mm(scatter, b_both))

    def far_wait(slot, c):
        at = recv_order[slot] * chunks + c

        def arrived(tiles):
            span = gathered.at[pl.ds(0, tiles)]
            pltpu.make_async_remote_copy(
                src_ref=span, dst_ref=span, send_sem=send_sem.at[0], recv_sem=recv_sem.at[at],
                device_id={"wide": above}, device_id_type=MESH,
            ).wait_recv()

        def wait():
            if slot > 0:
                arrived(group)
                return
            if group > 1:
                @pl.when(at == mine)
                def _():
                    arrived(group - 1)

            if chunks > 1:
                @pl.when(at != mine)
                def _():
                    arrived(group)

        wait()

    def far(slot, c):
        at = recv_order[slot] * chunks + c
        got = gathered[pl.ds(at * group, group)].reshape(group * rank_top, loads)
        b_both, b_high = pair(got)
        return product(u_high[at], u_low[at], b_both, b_high)

    out_ref[...] += scattered(1)
    order = [(slot, c) for slot in range(blocks) for c in range(chunks)]
    for step in order[:-1]:
        far_wait(*step)
        out_ref[...] += far(*step)

    def force_wait():
        @pl.when(has_below)
        def _():
            force_up.wait_recv()

        @pl.when(has_above)
        def _():
            force_down.wait_recv()

    far_wait(*order[-1])
    force_wait()
    out_ref[...] += far(*order[-1]) + (scattered(0) + scattered(2))

    def sent_wait():
        @pl.when(has_below)
        def _():
            pltpu.make_async_remote_copy(
                src_ref=edge_out.at[0], dst_ref=edge_out.at[0], send_sem=edge_send.at[0],
                recv_sem=face_recv.at[0], device_id={"wide": below}, device_id_type=MESH,
            ).wait_send()

        @pl.when(has_above)
        def _():
            pltpu.make_async_remote_copy(
                src_ref=edge_out.at[1], dst_ref=edge_out.at[1], send_sem=edge_send.at[1],
                recv_sem=face_recv.at[1], device_id={"wide": above}, device_id_type=MESH,
            ).wait_send()

        all_sent = sent.at[pl.ds(0, n - 1)]
        pltpu.make_async_remote_copy(
            src_ref=all_sent, dst_ref=all_sent, send_sem=send_sem.at[0], recv_sem=recv_sem.at[0],
            device_id={"wide": above}, device_id_type=MESH,
        ).wait_send()

    sent_wait()


def body(
    iterate, rhs, schur, near_block, u_basis, v_basis, tile_rank, send_rows, send_count, precond
):
    n = lax.axis_size("wide")
    rows_here, loads = iterate.shape
    face = send_rows.shape[2]
    tiles, rank_top, _ = u_basis.shape
    group = math.gcd(n // 4 if n % 4 == 0 else n, max(1, 128 // rank_top))
    tile_rank = tile_rank.reshape(1, tiles)
    send_rows = send_rows.reshape(3, 1, face)
    dma = pltpu.SemaphoreType.DMA
    applied = pl.pallas_call(
        functools.partial(kernel, n),
        out_shape=pltpu.VMEM((rows_here, loads), F32),
        in_specs=[pl.BlockSpec(memory_space=pl.ANY)] * 8,
        out_specs=pl.BlockSpec(memory_space=pltpu.VMEM),
        scratch_shapes=[
            pltpu.VMEM(iterate.shape, F32),
            pltpu.VMEM(schur.shape, F32),
            pltpu.VMEM(near_block.shape, F32),
            pltpu.VMEM(u_basis.shape, F32),
            pltpu.VMEM(v_basis.shape, F32),
            pltpu.SMEM(tile_rank.shape, jnp.int32),
            pltpu.VMEM(send_rows.shape, jnp.int32),
            pltpu.SMEM(send_count.shape, jnp.int32),
            pltpu.VMEM((2, 2, face, loads), F32),
            pltpu.VMEM((3, face, loads), F32),
            pltpu.VMEM((3, face, loads), F32),
            pltpu.VMEM((n, rank_top, loads), F32),
            pltpu.VMEM((n, rank_top, loads), F32),
            pltpu.VMEM((n // group, rows_here, group * rank_top), BF16),
            pltpu.VMEM((n // group, rows_here, group * rank_top), BF16),
            dma((3 + n // group,)),
            dma((2,)),
            dma((2,)),
            dma((2,)),
            dma((1,)),
            dma((n // group,)),
            pltpu.SemaphoreType.REGULAR((2,)),
        ],
        compiler_params=pltpu.CompilerParams(collective_id=0, has_side_effects=True),
    )(iterate, schur, near_block, u_basis, v_basis, tile_rank, send_rows, send_count)
    residual = rhs - applied
    updated = iterate + precond[:, None] * residual
    return (updated, residual)


def solution(mesh):
    in_specs = (
        P(("groups", "wide"), None),
        P(("groups", "wide"), None),
        P(("groups", "wide"), None, None),
        P(("groups", "wide"), None),
        P("groups", None, "wide"),
        P("groups", None, "wide"),
        P("groups", "wide"),
        P(("groups", "wide"), None, None),
        P(("groups", "wide"), None),
        P(("groups", "wide")),
    )
    out_specs = (P(("groups", "wide"), None), P(("groups", "wide"), None))
    return jax.shard_map(body, mesh=mesh, in_specs=in_specs, out_specs=out_specs, check_vma=False)
```
